512 devices in a mesh: dp: 64 (over z, y), group: 8 (over x, core).
Axes of the slice: x: 4, y: 8, z: 8, core: 2. Of those that a mesh axis runs over, the one named last changes fastest.
Arguments:
- rewards: float32 [8192, 4096], P(('dp', 'group')), may hold values from -6 to 6
- values: float32 [8192, 4096], P(('dp', 'group')), may hold values from -6 to 6
- horizon: float32 [8192], P(('dp', 'group')), may hold values from 16 to 32768
- lengths: int32 [8192], P(('dp', 'group')), may hold values from 1 to 4096
- assignment: int32 [64, 4096], P('dp', 'group'), may hold values from 0 to 4095, as said below
Outputs:
- returns: float32 [8192, 4096], P(('dp', 'group'))
- train_adv: float32 [262144, 128], P(('dp', 'group'))
The draws below stay inside these ranges and needn't reach their ends.
Inputs may be any that keep to these rules, and one draw needn't show every extreme that they name: Each row of assignment names each of the 4096 blocks of its index of dp once; the slots held by one device take at most 128 blocks from the sequences of any one device of its group, and that most is reached in every row.
All inputs are finite; a program needn't handle non-finite values.
Results may differ from the reference program's by a relative error of at most 0.0001.
Values sent between devices are 32-bit elements; how exact they have to be, the bound alone decides.
A program may use at most 64 MiB of HBM per device.

```python
import math
import jax
import jax.numpy as jnp
from jax import lax

LEN = 4096
BLK = 128
SEQS = 8192
GBLK = 4096
N_DP = 64
N_GROUP = 8


def assign_row(key):
    per_dev = GBLK // N_GROUP
    quota = per_dev // N_GROUP
    key_a, key_b, key_p, key_n = jax.random.split(key, 4)
    first = jax.random.randint(key_a, (), 0, N_GROUP, dtype=jnp.int32)
    second = (first + jax.random.randint(key_b, (), 1, N_GROUP, dtype=jnp.int32)) % N_GROUP
    source = jnp.arange(N_GROUP, dtype=jnp.int32)[:, None]
    target = jnp.arange(N_GROUP, dtype=jnp.int32)[None, :]
    plus = (target == (source + first) % N_GROUP).astype(jnp.int32)
    minus = (target == (source + second) % N_GROUP).astype(jnp.int32)
    counts = quota + quota * (plus - minus)
    ends = jnp.cumsum(counts, axis=1)
    place = jnp.arange(per_dev, dtype=jnp.int32)
    dest_of = jnp.sum((place[None, :, None] >= ends[:, None, :]).astype(jnp.int32), axis=2)
    perm_keys = jax.random.split(key_p, N_GROUP)
    perms = jax.vmap(lambda k: jax.random.permutation(k, per_dev))(perm_keys).astype(jnp.int32)
    block_ids = source * per_dev + perms
    dest_block = jnp.zeros((GBLK,), jnp.int32).at[block_ids.reshape(-1)].set(dest_of.reshape(-1))
    noise = jax.random.permutation(key_n, GBLK).astype(jnp.int32)
    order_keys = dest_block * GBLK + noise
    return jnp.argsort(order_keys, stable=True).astype(jnp.int32)


def draw_assignment(key, part):
    keys = jax.random.split(jax.random.fold_in(key, 7), N_DP)
    return jax.vmap(assign_row)(keys)


def plant(drawn, own_key, low, largest):
    shape = drawn.shape
    spot = [jax.random.randint(jax.random.fold_in(own_key, axis), (), 0, shape[axis]) for axis in range(len(shape))]
    drawn = drawn.at[tuple(spot)].set(low)
    longest = shape.index(max(shape))
    spot[longest] = (spot[longest] + 1) % shape[longest]
    return drawn.at[tuple(spot)].set(largest)


def level_of(rng, shape, pieces, low, high):
    loudness = 1.0
    for axis_at, shards_of in pieces:
        heights = jax.random.uniform(jax.random.fold_in(jax.random.fold_in(rng, 6), axis_at), (shards_of,), jnp.float32, low / len(pieces), high / len(pieces))
        loudness = loudness * jnp.repeat(jnp.exp(heights), shape[axis_at] // shards_of).reshape((-1,) + (1,) * (len(shape) - 1 - axis_at))
    return loudness


def gaussian(stream_key, dims, scale, most, cuts=(), held_as=jnp.bfloat16):
    values = scale * jax.random.normal(stream_key, dims, jnp.float32)
    if cuts:
        values = values * level_of(stream_key, dims, cuts, -0.22, 0.18)
    return jnp.clip(values, -most, most).astype(held_as)


def setup_inputs(seed: int = 0) -> dict:
    splits = jax.random.split(jax.random.key(seed), 6)
    rewards = gaussian(splits[0], (SEQS, LEN), 1.0, 6.0, ((0, 512),), jnp.float32)
    values = gaussian(splits[1], (SEQS, LEN), 1.0, 6.0, ((0, 512),), jnp.float32)
    horizon = jnp.clip(jnp.exp(math.log(32768.0) - 7.624619 * jax.random.uniform(splits[2], (SEQS,), jnp.float32) ** level_of(splits[2], (SEQS,), ((0, 512),), -0.2, 0.2)), 16.0, 32768.0)
    lengths = plant(jax.random.randint(splits[3], (SEQS,), 1, LEN + 1), jax.random.fold_in(splits[3], 1), 1, LEN).astype(jnp.int32)
    assignment = draw_assignment(jax.random.fold_in(splits[5], 71), 0)
    return {"rewards": rewards, "values": values, "horizon": horizon, "lengths": lengths, "assignment": assignment}


trace_decay = 0.998
epsilon = 1e-05

def reference(rewards, values, horizon, lengths, assignment):
    gamma = 1.0 - 1.0 / horizon
    coeff = gamma * trace_decay
    position = jnp.arange(LEN, dtype=jnp.int32)
    inside = position[None, :] < lengths[:, None]
    follows = position[None, :] + 1 < lengths[:, None]
    shifted = jnp.concatenate([values[:, 1:], jnp.zeros((SEQS, 1), values.dtype)], axis=1)
    upcoming = jnp.where(follows, shifted, 0.0)
    deltas = jnp.where(inside, rewards + gamma[:, None] * upcoming - values, 0.0)

    def backward(carry, column):
        value_now = column + coeff * carry
        return (value_now, value_now)
    _, advantage = lax.scan(backward, jnp.zeros((SEQS,), rewards.dtype), deltas.T, reverse=True)
    advantage = advantage.T
    returns = jnp.where(inside, advantage + values, 0.0)
    weight = inside.astype(rewards.dtype)
    counted = jnp.sum(weight)
    center = jnp.sum(advantage * weight) / counted
    spread = jnp.sum(weight * (advantage - center) ** 2)
    scale = lax.rsqrt(spread / counted + epsilon)
    whitened = jnp.where(inside, (advantage - center) * scale, 0.0)
    blocks = whitened.reshape(N_DP, GBLK, BLK)
    chosen = jnp.take_along_axis(blocks, assignment.astype(jnp.int32)[:, :, None], axis=1)
    return (returns, chosen.reshape(N_DP * GBLK, BLK))
```

```python
import jax
import jax.numpy as jnp
from jax import lax
from jax.experimental import pallas as pl
from jax.experimental.pallas import tpu as pltpu
from jax.sharding import PartitionSpec as P

LEN = 4096
BLK = 128
SEQ = 16
NBLK = LEN // BLK
ROWS = SEQ * NBLK
HALF = ROWS // 2
TRACE_DECAY = 0.998
EPSILON = 1e-05
OUTSIDE = 1e30
LIMIT = 1e29
CHUNK = 8
MESH = pl.DeviceIdType.MESH


def column(row):
    wide = jnp.broadcast_to(row, (SEQ, SEQ))
    down = lax.broadcasted_iota(jnp.int32, (SEQ, SEQ), 0)
    across = lax.broadcasted_iota(jnp.int32, (SEQ, SEQ), 1)
    picked = jnp.sum(jnp.where(down == across, wide, 0.0), axis=1, keepdims=True)
    return jnp.broadcast_to(picked, (SEQ, BLK))


def merged(buf):
    n, m, s = buf[:, 0, :], buf[:, 1, :], buf[:, 2, :]
    total = jnp.sum(n, axis=0, keepdims=True)
    mean = jnp.sum(n * m, axis=0, keepdims=True) / total
    gap = m - mean
    spread = jnp.sum(s + n * gap * gap, axis=0, keepdims=True)
    return total, mean, spread


def kernel(rew_hbm, val_hbm, hor_hbm, len_hbm, asg_hbm, ret_hbm, train_hbm,
           rew, val, hor, lens, asg, ret, gath, rows, mom,
           in_sem, out_sem, mom_send, mom_recv, data_send, data_recv):
    d = lax.axis_index("dp")
    g = lax.axis_index("group")
    y, z = lax.rem(d, 8), d // 8
    group_peers = [(d, lax.rem(g + k, 8)) for k in range(1, 8)]
    y_peers = [(z * 8 + lax.rem(y + k, 8), g) for k in range(1, 8)]
    z_peers = [(lax.rem(d + 8 * k, 64), g) for k in range(1, 8)]

    barrier = pltpu.get_barrier_semaphore()
    for peer in z_peers + y_peers + group_peers:
        pl.semaphore_signal(barrier, inc=1, device_id=peer, device_id_type=MESH)

    loads = [
        pltpu.make_async_copy(src, dst, in_sem.at[i])
        for i, (src, dst) in enumerate(
            [(hor_hbm, hor), (len_hbm, lens), (val_hbm, val), (rew_hbm, rew), (asg_hbm, asg)])
    ]
    for load in loads:
        load.start()
    for load in loads[:4]:
        load.wait()

    lane = lax.broadcasted_iota(jnp.int32, (SEQ, BLK), 1)
    length = column(lens[...].astype(jnp.float32)).astype(jnp.int32)
    gamma = 1.0 - 1.0 / column(hor[...])
    powers = [gamma * TRACE_DECAY]
    for _ in range(7):
        powers.append(powers[-1] * powers[-1])
    steps = [jnp.where(lane < BLK - (1 << k), powers[k], 0.0) for k in range(7)]
    togo = BLK - lane
    tail = jnp.where(togo == BLK, powers[7], 1.0)
    for k in range(7):
        tail = tail * jnp.where(((togo >> k) & 1) == 1, powers[k], 1.0)

    zero = jnp.zeros((SEQ, BLK), jnp.float32)
    carry, ahead, total = zero, zero, zero
    shape = (CHUNK, SEQ, BLK)
    for first in range(NBLK - CHUNK, -1, -CHUNK):
        cols = [slice((first + i) * BLK, (first + i + 1) * BLK) for i in range(CHUNK)]
        v = jnp.stack([val[:, c] for c in cols])
        r = jnp.stack([rew[:, c] for c in cols])
        turned = pltpu.roll(v, BLK - 1, 2)
        following = jnp.concatenate([turned[1:], ahead[None]], axis=0)
        ahead = turned[0]
        shifted = jnp.where(lane[None] < BLK - 1, turned, following)
        block = lax.broadcasted_iota(jnp.int32, shape, 0) + first
        left = length[None] - block * BLK
        inside = lane[None] < left
        follows = lane[None] + 1 < left
        part = jnp.where(inside, r + gamma[None] * jnp.where(follows, shifted, 0.0) - v, 0.0)
        for k in range(7):
            part = part + steps[k][None] * pltpu.roll(part, BLK - (1 << k), 2)
        head = jnp.broadcast_to(part[:, :, 0:1], shape)
        for i in range(CHUNK - 1, -1, -1):
            adv = part[i] + tail * carry
            carry = head[i] + powers[7] * carry
            total = total + adv
            ret[:, cols[i]] = jnp.where(inside[i], adv + v[i], 0.0)
            sent = jnp.where(inside[i], adv, OUTSIDE)
            at = (first + i) * 8
            gath[g, at:at + 8, :] = sent[:8]
            gath[g, HALF + at:HALF + at + 8, :] = sent[8:]
    give_returns = pltpu.make_async_copy(ret, ret_hbm, out_sem.at[0])
    give_returns.start()

    count = jnp.sum(jnp.sum(length[:, 0:1].astype(jnp.float32), axis=0, keepdims=True), axis=1, keepdims=True)
    mean = jnp.sum(jnp.sum(total, axis=0, keepdims=True), axis=1, keepdims=True) / count
    square = jnp.zeros((8, BLK), jnp.float32)
    for i in range(ROWS // 64):
        own = gath[g, i * 64:(i + 1) * 64, :]
        gap = jnp.where(own < LIMIT, own - mean, 0.0)
        square = square + jnp.sum((gap * gap).reshape(8, 8, BLK), axis=0)
    spread = jnp.sum(jnp.sum(square, axis=0, keepdims=True), axis=1, keepdims=True)

    def stage_send(stage, triple, peers):
        for j in range(3):
            mom[stage, 0, j:j + 1, :] = jnp.broadcast_to(triple[j], (1, BLK))
        copies = []
        for k, peer in enumerate(peers, 1):
            copy = pltpu.make_async_remote_copy(
                src_ref=mom.at[stage, 0, 0:3], dst_ref=mom.at[stage, k, 0:3],
                send_sem=mom_send.at[stage, k], recv_sem=mom_recv.at[stage, k],
                device_id=peer, device_id_type=MESH)
            copy.start()
            copies.append(copy)
        return copies

    def stage_wait(stage, copies):
        for copy in copies:
            copy.wait_recv()
        return merged(mom[stage])

    pl.semaphore_wait(barrier, 21)
    at_group = stage_send(0, (count, mean, spread), group_peers)

    mate = g + 1 - 2 * lax.rem(g, 2)
    right, left, far = lax.rem(g + 2, 8), lax.rem(g + 6, 8), lax.rem(g + 4, 8)
    low, high, whole = pl.ds(0, HALF), pl.ds(HALF, HALF), pl.ds(0, ROWS)

    def move(i, owner, span, to):
        copy = pltpu.make_async_remote_copy(
            src_ref=gath.at[owner, span], dst_ref=gath.at[owner, span],
            send_sem=data_send.at[i], recv_sem=data_recv.at[i],
            device_id=(d, to), device_id_type=MESH)
        copy.start()
        return copy

    r1 = move(0, g, low, right)
    l1 = move(1, g, high, left)
    r2 = move(2, g, high, right)
    l2 = move(3, g, low, left)
    own = move(4, g, whole, mate)

    to_y = stage_send(1, stage_wait(0, at_group), y_peers)

    r1.wait_recv()
    r3 = move(5, left, low, right)
    l1.wait_recv()
    l3 = move(6, right, high, left)
    m1 = move(7, left, low, mate)
    m2 = move(8, right, high, mate)

    to_z = stage_send(2, stage_wait(1, to_y), z_peers)

    r2.wait_recv()
    m3 = move(9, left, high, mate)
    l2.wait_recv()
    m4 = move(10, right, low, mate)
    r3.wait_recv()
    m5 = move(11, far, low, mate)
    l3.wait_recv()
    m6 = move(12, far, high, mate)
    for copy in (own, m1, m2, m3, m4, m5, m6):
        copy.wait_recv()

    loads[4].wait()

    def gather(i, _):
        for j in range(16):
            slot = i * 16 + j
            want = asg[0, slot]
            row = ((want & 31) << 3) | ((want >> 5) & 7)
            rows[pl.ds(slot, 1), :] = gath[want >> 9, pl.ds((want & 256) + row, 1), :]
        return 0

    lax.fori_loop(0, ROWS // 16, gather, 0)

    n, middle, deviation = stage_wait(2, to_z)
    scale = lax.rsqrt(deviation / n + EPSILON)
    picked = rows[...]
    rows[...] = jnp.where(picked < LIMIT, (picked - middle) * scale, 0.0)
    give_train = pltpu.make_async_copy(rows, train_hbm, out_sem.at[1])
    give_train.start()

    for copy in at_group + to_y + to_z + [r1, l1, r2, l2, own, r3, l3, m1, m2, m3, m4, m5, m6]:
        copy.wait_send()
    give_returns.wait()
    give_train.wait()


def body(rewards, values, horizon, lengths, assignment):
    hbm = pl.BlockSpec(memory_space=pltpu.MemorySpace.HBM)
    f32 = jnp.float32
    return pl.pallas_call(
        kernel,
        out_shape=(jax.ShapeDtypeStruct((SEQ, LEN), f32), jax.ShapeDtypeStruct((ROWS, BLK), f32)),
        in_specs=[hbm] * 5,
        out_specs=(hbm, hbm),
        scratch_shapes=[
            pltpu.VMEM((SEQ, LEN), f32),
            pltpu.VMEM((SEQ, LEN), f32),
            pltpu.VMEM((1, SEQ), f32),
            pltpu.VMEM((1, SEQ), jnp.int32),
            pltpu.SMEM((1, ROWS), jnp.int32),
            pltpu.VMEM((SEQ, LEN), f32),
            pltpu.VMEM((8, ROWS, BLK), f32),
            pltpu.VMEM((ROWS, BLK), f32),
            pltpu.VMEM((3, 8, 8, BLK), f32),
            pltpu.SemaphoreType.DMA((5,)),
            pltpu.SemaphoreType.DMA((2,)),
            pltpu.SemaphoreType.DMA((3, 8)),
            pltpu.SemaphoreType.DMA((3, 8)),
            pltpu.SemaphoreType.DMA((13,)),
            pltpu.SemaphoreType.DMA((13,)),
        ],
        compiler_params=pltpu.CompilerParams(collective_id=0, has_side_effects=True),
        name="advantage",
    )(rewards, values, horizon.reshape(1, SEQ), lengths.reshape(1, SEQ), assignment)


def solution(mesh):
    in_specs = (
        P(("dp", "group"), None),
        P(("dp", "group"), None),
        P(("dp", "group")),
        P(("dp", "group")),
        P("dp", "group"),
    )
    out_specs = (P(("dp", "group"), None), P(("dp", "group"), None))
    return jax.shard_map(body, mesh=mesh, in_specs=in_specs, out_specs=out_specs, check_vma=False)
```

```python
import jax
import jax.numpy as jnp
from jax import lax
from jax.experimental import pallas as pl
from jax.experimental.pallas import tpu as pltpu
from jax.sharding import PartitionSpec as P

LEN = 4096
BLK = 128
SEQ = 16
NBLK = LEN // BLK
ROWS = SEQ * NBLK
HALF = ROWS // 2
TRACE_DECAY = 0.998
EPSILON = 1e-05
OUTSIDE = 1e30
LIMIT = 1e29
CHUNK = 8
MESH = pl.DeviceIdType.MESH


def column(row):
    wide = jnp.broadcast_to(row, (SEQ, SEQ))
    down = lax.broadcasted_iota(jnp.int32, (SEQ, SEQ), 0)
    across = lax.broadcasted_iota(jnp.int32, (SEQ, SEQ), 1)
    picked = jnp.sum(jnp.where(down == across, wide, 0.0), axis=1, keepdims=True)
    return jnp.broadcast_to(picked, (SEQ, BLK))


def as_row(count, mean, spread):
    lane = lax.broadcasted_iota(jnp.int32, (1, BLK), 1)
    return jnp.where(lane == 0, count, jnp.where(lane == 1, mean, spread))


def merged(rows):
    n, m, s = (jnp.broadcast_to(rows[:, j:j + 1], rows.shape) for j in range(3))
    total = jnp.sum(n, axis=0, keepdims=True)
    mean = jnp.sum(n * m, axis=0, keepdims=True) / total
    gap = m - mean
    spread = jnp.sum(s + n * gap * gap, axis=0, keepdims=True)
    return total, mean, spread


def each(first, last, act):
    lax.fori_loop(first, last, lambda k, c: (act(k), c)[1], 0)


def kernel(rew_hbm, val_hbm, hor_hbm, len_hbm, asg_hbm, ret, rows, stats,
           rew, val, hor, lens, asg, gath, plane, line,
           in_sem, plane_sem, z_sem, here, data_send, data_recv):
    d = lax.axis_index("dp")
    g = lax.axis_index("group")
    y, z = lax.rem(d, 8), d // 8

    def signal(sem, where):
        pl.semaphore_signal(sem, inc=1, device_id=where, device_id_type=MESH)

    def await_signals(sem, count):
        @pl.when(count > 0)
        def _():
            pl.semaphore_wait(sem, count)

    def on_line(k):
        return k * 8 + y, g

    def on_row(k):
        return z * 8 + k, g

    def on_plane(k):
        return z * 8 + k // 8, lax.rem(k, 8)

    loads = [
        pltpu.make_async_copy(src, dst, in_sem.at[i])
        for i, (src, dst) in enumerate(
            [(hor_hbm, hor), (len_hbm, lens), (val_hbm, val), (rew_hbm, rew), (asg_hbm, asg)])
    ]
    for load in loads:
        load.start()
    barrier = pltpu.get_barrier_semaphore()
    for k in range(1, 8):
        signal(barrier, (d, lax.rem(g + k, 8)))
    each(z + 1, 8, lambda k: signal(barrier, on_line(k)))
    each(y + 1, 8, lambda k: signal(barrier, on_row(k)))

    for load in loads[:4]:
        load.wait()

    lane = lax.broadcasted_iota(jnp.int32, (SEQ, BLK), 1)
    length = column(lens[...].astype(jnp.float32)).astype(jnp.int32)
    gamma = 1.0 - 1.0 / column(hor[...])
    powers = [gamma * TRACE_DECAY]
    for _ in range(7):
        powers.append(powers[-1] * powers[-1])
    steps = [jnp.where(lane < BLK - (1 << k), powers[k], 0.0) for k in range(7)]
    togo = BLK - lane
    tail = jnp.where(togo == BLK, powers[7], 1.0)
    for k in range(7):
        tail = tail * jnp.where(((togo >> k) & 1) == 1, powers[k], 1.0)

    zero = jnp.zeros((SEQ, BLK), jnp.float32)
    carry, ahead, total = zero, zero, zero
    shape = (CHUNK, SEQ, BLK)
    for first in range(NBLK - CHUNK, -1, -CHUNK):
        cols = [slice((first + i) * BLK, (first + i + 1) * BLK) for i in range(CHUNK)]
        v = jnp.stack([val[:, c] for c in cols])
        r = jnp.stack([rew[:, c] for c in cols])
        turned = pltpu.roll(v, BLK - 1, 2)
        following = jnp.concatenate([turned[1:], ahead[None]], axis=0)
        ahead = turned[0]
        shifted = jnp.where(lane[None] < BLK - 1, turned, following)
        block = lax.broadcasted_iota(jnp.int32, shape, 0) + first
        left = length[None] - block * BLK
        inside = lane[None] < left
        follows = lane[None] + 1 < left
        part = jnp.where(inside, r + gamma[None] * jnp.where(follows, shifted, 0.0) - v, 0.0)
        for k in range(7):
            part = part + steps[k][None] * pltpu.roll(part, BLK - (1 << k), 2)
        head = jnp.broadcast_to(part[:, :, 0:1], shape)
        for i in range(CHUNK - 1, -1, -1):
            adv = part[i] + tail * carry
            carry = head[i] + powers[7] * carry
            total = total + adv
            ret[:, cols[i]] = jnp.where(inside[i], adv + v[i], 0.0)
            sent = jnp.where(inside[i], adv, OUTSIDE)
            at = (first + i) * 8
            gath[g, at:at + 8, :] = sent[:8]
            gath[g, HALF + at:HALF + at + 8, :] = sent[8:]

    count = jnp.sum(jnp.sum(length[:, 0:1].astype(jnp.float32), axis=0, keepdims=True), axis=1, keepdims=True)
    mean = jnp.sum(jnp.sum(total, axis=0, keepdims=True), axis=1, keepdims=True) / count
    square = jnp.zeros((8, BLK), jnp.float32)
    for i in range(ROWS // 64):
        own = gath[g, i * 64:(i + 1) * 64, :]
        gap = jnp.where(own < LIMIT, own - mean, 0.0)
        square = square + jnp.sum((gap * gap).reshape(8, 8, BLK), axis=0)
    spread = jnp.sum(jnp.sum(square, axis=0, keepdims=True), axis=1, keepdims=True)

    line[pl.ds(z, 1), :] = as_row(count, mean, spread)
    pl.semaphore_wait(barrier, 7 + z + y)

    def send(buf, slot, sem, to):
        pltpu.make_async_remote_copy(
            src_ref=buf.at[pl.ds(slot, 1)], dst_ref=buf.at[pl.ds(slot, 1)],
            send_sem=sem.at[0], recv_sem=sem.at[1],
            device_id=to, device_id_type=MESH).start()

    def send_line(k):
        send(line, z, z_sem, on_line(k))

    each(0, z, send_line)
    each(0, z, lambda k: signal(here.at[0], on_line(k)))

    mate = g + 1 - 2 * lax.rem(g, 2)
    right, left, far = lax.rem(g + 2, 8), lax.rem(g + 6, 8), lax.rem(g + 4, 8)
    low, high, whole = pl.ds(0, HALF), pl.ds(HALF, HALF), pl.ds(0, ROWS)

    def move(i, owner, span, to):
        copy = pltpu.make_async_remote_copy(
            src_ref=gath.at[owner, span], dst_ref=gath.at[owner, span],
            send_sem=data_send.at[i], recv_sem=data_recv.at[i],
            device_id=(d, to), device_id_type=MESH)
        copy.start()
        return copy

    r1 = move(0, g, low, right)
    l1 = move(1, g, high, left)
    r2 = move(2, g, high, right)
    l2 = move(3, g, low, left)
    own = move(4, g, whole, mate)

    each(0, y, lambda k: signal(here.at[1], on_row(k)))

    r1.wait_recv()
    r3 = move(5, left, low, right)
    l1.wait_recv()
    l3 = move(6, right, high, left)
    m1 = move(7, left, low, mate)
    m2 = move(8, right, high, mate)
    await_signals(here.at[1], 7 - y)
    each(y + 1, 8, lambda k: signal(here.at[2], on_row(k)))
    await_signals(here.at[0], 7 - z)
    each(z + 1, 8, send_line)
    others_z = line.at[pl.ds(0, 7)]
    pltpu.make_async_copy(others_z, others_z, z_sem.at[1]).wait()
    mine = y * 8 + g
    plane[pl.ds(mine, 1), :] = as_row(*merged(line[...]))
    await_signals(here.at[2], y)
    each(1, 64, lambda k: send(plane, mine, plane_sem, on_plane(lax.rem(mine + k, 64))))

    r2.wait_recv()
    m3 = move(9, left, high, mate)
    l2.wait_recv()
    m4 = move(10, right, low, mate)

    r3.wait_recv()
    m5 = move(11, far, low, mate)
    l3.wait_recv()
    m6 = move(12, far, high, mate)
    for copy in (own, m1, m2, m3, m4, m5, m6):
        copy.wait_recv()

    loads[4].wait()

    def gather(i, _):
        for j in range(16):
            slot = i * 16 + j
            want = asg[0, slot]
            row = ((want & 31) << 3) | ((want >> 5) & 7)
            rows[pl.ds(slot, 1), :] = gath[want >> 9, pl.ds((want & 256) + row, 1), :]
        return 0

    lax.fori_loop(0, ROWS // 16, gather, 0)

    others = plane.at[pl.ds(0, 63)]
    pltpu.make_async_copy(others, others, plane_sem.at[1]).wait()
    n, middle, deviation = merged(plane[...])
    stats[0:1, :] = middle
    stats[1:2, :] = lax.rsqrt(deviation / n + EPSILON)
    pltpu.make_async_copy(others, others, plane_sem.at[0]).wait()
    pltpu.make_async_copy(others_z, others_z, z_sem.at[0]).wait()
    for copy in [r1, l1, r2, l2, own, r3, l3, m1, m2, m3, m4, m5, m6]:
        copy.wait_send()


def finish(ret, rows, stats, ret_hbm, train_hbm, train, sem):
    give_returns = pltpu.make_async_copy(ret, ret_hbm, sem.at[0])
    give_returns.start()
    middle, scale = stats[0:1, :], stats[1:2, :]
    gives = []
    for i in range(2):
        part = slice(i * HALF, (i + 1) * HALF)
        picked = rows[part, :]
        train[part, :] = jnp.where(picked < LIMIT, (picked - middle) * scale, 0.0)
        give = pltpu.make_async_copy(train.at[part], train_hbm.at[part], sem.at[1 + i])
        give.start()
        gives.append(give)
    give_returns.wait()
    for give in gives:
        give.wait()


def body(rewards, values, horizon, lengths, assignment):
    hbm = pl.BlockSpec(memory_space=pltpu.MemorySpace.HBM)
    f32 = jnp.float32
    vmem = pl.BlockSpec(memory_space=pltpu.MemorySpace.VMEM)
    ret, rows, stats = pl.pallas_call(
        kernel,
        out_shape=tuple(jax.ShapeDtypeStruct(shape, f32) for shape in ((SEQ, LEN), (ROWS, BLK), (8, BLK))),
        in_specs=[hbm] * 5,
        out_specs=(vmem, vmem, vmem),
        scratch_shapes=[
            pltpu.VMEM((SEQ, LEN), f32),
            pltpu.VMEM((SEQ, LEN), f32),
            pltpu.VMEM((1, SEQ), f32),
            pltpu.VMEM((1, SEQ), jnp.int32),
            pltpu.SMEM((1, ROWS), jnp.int32),
            pltpu.VMEM((8, ROWS, BLK), f32),
            pltpu.VMEM((64, BLK), f32),
            pltpu.VMEM((8, BLK), f32),
            pltpu.SemaphoreType.DMA((5,)),
            pltpu.SemaphoreType.DMA((2,)),
            pltpu.SemaphoreType.DMA((2,)),
            pltpu.SemaphoreType.REGULAR((3,)),
            pltpu.SemaphoreType.DMA((13,)),
            pltpu.SemaphoreType.DMA((13,)),
        ],
        compiler_params=pltpu.CompilerParams(collective_id=0, has_side_effects=True, vmem_limit_bytes=16 << 20),
        name="advantage",
    )(*(pltpu.with_memory_space_constraint(x, pltpu.MemorySpace.HBM) for x in (rewards, values, horizon.reshape(1, SEQ), lengths.reshape(1, SEQ), assignment)))
    return pl.pallas_call(
        finish,
        out_shape=(jax.ShapeDtypeStruct((SEQ, LEN), f32), jax.ShapeDtypeStruct((ROWS, BLK), f32)),
        in_specs=[vmem] * 3,
        out_specs=(hbm, hbm),
        scratch_shapes=[pltpu.VMEM((ROWS, BLK), f32), pltpu.SemaphoreType.DMA((3,))],
        compiler_params=pltpu.CompilerParams(vmem_limit_bytes=4 << 20),
        name="finish",
    )(ret, rows, stats)


def solution(mesh):
    in_specs = (
        P(("dp", "group"), None),
        P(("dp", "group"), None),
        P(("dp", "group")),
        P(("dp", "group")),
        P("dp", "group"),
    )
    out_specs = (P(("dp", "group"), None), P(("dp", "group"), None))
    return jax.shard_map(body, mesh=mesh, in_specs=in_specs, out_specs=out_specs, check_vma=False)
```

```python
import jax
import jax.numpy as jnp
from jax import lax
from jax.experimental import pallas as pl
from jax.experimental.pallas import tpu as pltpu
from jax.sharding import PartitionSpec as P

LEN = 4096
BLK = 128
SEQ = 16
NBLK = LEN // BLK
ROWS = SEQ * NBLK
HALF = ROWS // 2
TRACE_DECAY = 0.998
MORE = 1.0 / TRACE_DECAY - 1.0
EPSILON = 1e-05
OUTSIDE = 1e30
LIMIT = 1e29
CHUNK = 8
MESH = pl.DeviceIdType.MESH


def column(row):
    wide = jnp.broadcast_to(row, (SEQ, SEQ))
    down = lax.broadcasted_iota(jnp.int32, (SEQ, SEQ), 0)
    across = lax.broadcasted_iota(jnp.int32, (SEQ, SEQ), 1)
    picked = jnp.sum(jnp.where(down == across, wide, 0.0), axis=1, keepdims=True)
    return jnp.broadcast_to(picked, (SEQ, BLK))


def as_row(count, mean, spread):
    lane = lax.broadcasted_iota(jnp.int32, (1, BLK), 1)
    return jnp.where(lane == 0, count, jnp.where(lane == 1, mean, spread))


def merged(rows):
    n, m, s = (jnp.broadcast_to(rows[:, j:j + 1], rows.shape) for j in range(3))
    total = jnp.sum(n, axis=0, keepdims=True)
    mean = jnp.sum(n * m, axis=0, keepdims=True) / total
    gap = m - mean
    spread = jnp.sum(s + n * gap * gap, axis=0, keepdims=True)
    return total, mean, spread


def each(first, last, act):
    lax.fori_loop(first, last, lambda k, c: (act(k), c)[1], 0)


def kernel(rew_hbm, val_hbm, hor_hbm, len_hbm, asg_hbm, ret, rows, stats,
           rew, val, hor, lens, asg, gath, plane, line,
           in_sem, plane_sem, z_sem, here, data_send, data_recv):
    d = lax.axis_index("dp")
    g = lax.axis_index("group")
    y, z = lax.rem(d, 8), d // 8

    def signal(sem, where):
        pl.semaphore_signal(sem, inc=1, device_id=where, device_id_type=MESH)

    def await_signals(sem, count):
        @pl.when(count > 0)
        def _():
            pl.semaphore_wait(sem, count)

    def on_line(k):
        return k * 8 + y, g

    def on_row(k):
        return z * 8 + k, g

    def on_plane(k):
        return z * 8 + k // 8, lax.rem(k, 8)

    loads = [
        pltpu.make_async_copy(src, dst, in_sem.at[i])
        for i, (src, dst) in enumerate(
            [(hor_hbm, hor), (len_hbm, lens), (val_hbm, val), (rew_hbm, rew), (asg_hbm, asg)])
    ]
    for load in loads:
        load.start()

    barrier = pltpu.get_barrier_semaphore()
    for k in range(1, 8):
        signal(barrier, (d, lax.rem(g + k, 8)))
    each(z + 1, 8, lambda k: signal(barrier, on_line(k)))
    each(y + 1, 8, lambda k: signal(barrier, on_row(k)))

    loads[0].wait()
    loads[1].wait()

    lane = lax.broadcasted_iota(jnp.int32, (SEQ, BLK), 1)
    length = column(lens[...].astype(jnp.float32)).astype(jnp.int32)
    gamma = 1.0 - 1.0 / column(hor[...])
    power = gamma * TRACE_DECAY
    rise = jnp.ones((SEQ, BLK), jnp.float32)
    for k in range(7):
        rise = rise * jnp.where(((lane >> k) & 1) == 1, power, 1.0)
        power = power * power
    fall = 1.0 / rise
    down = lax.broadcasted_iota(jnp.int32, (BLK, 2 * BLK), 0)
    across = lax.broadcasted_iota(jnp.int32, (BLK, 2 * BLK), 1)
    ones = jnp.where((across >= BLK) | (down >= across), 1.0, 0.0).astype(jnp.bfloat16)
    twice = jnp.concatenate([ones, ones], axis=0)
    past = lane - length
    zero = jnp.zeros((SEQ, BLK), jnp.float32)
    carry, total = zero, zero
    shape = (CHUNK, SEQ, BLK)
    loads[2].wait()
    loads[3].wait()
    for first in range(NBLK - CHUNK, -1, -CHUNK):
        cols = [slice((first + i) * BLK, (first + i + 1) * BLK) for i in range(CHUNK)]
        v = jnp.stack([val[:, c] for c in cols])
        r = jnp.stack([rew[:, c] for c in cols])
        inside = jnp.stack([past < -(first + i) * BLK for i in range(CHUNK)])
        part = jnp.where(inside, r + MORE * v, 0.0)
        scaled = (part * rise[None]).reshape(CHUNK * SEQ, BLK)
        high = scaled.astype(jnp.bfloat16)
        rest = scaled - high.astype(jnp.float32)
        middle = rest.astype(jnp.bfloat16)
        low = (rest - middle.astype(jnp.float32)).astype(jnp.bfloat16)
        sums = jnp.dot(jnp.concatenate([high, middle], axis=1), twice, preferred_element_type=jnp.float32)
        sums = sums + jnp.dot(low, ones, preferred_element_type=jnp.float32)
        inner, whole_block = sums[:, :BLK].reshape(shape), sums[:, BLK:].reshape(shape)
        for i in range(CHUNK - 1, -1, -1):
            tail = power * carry
            adv = (inner[i] + tail) * fall - (1.0 + MORE) * v[i]
            carry = whole_block[i] + tail
            total = total + jnp.where(inside[i], adv, 0.0)
            sent = jnp.where(inside[i], adv, OUTSIDE)
            at = (first + i) * 8
            gath[g, at:at + 8, :] = sent[:8]
            gath[g, HALF + at:HALF + at + 8, :] = sent[8:]

    count = jnp.sum(jnp.sum(length[:, 0:1].astype(jnp.float32), axis=0, keepdims=True), axis=1, keepdims=True)
    mean = jnp.sum(jnp.sum(total, axis=0, keepdims=True), axis=1, keepdims=True) / count
    square = jnp.zeros((8, BLK), jnp.float32)
    for i in range(ROWS // 64):
        own = gath[g, i * 64:(i + 1) * 64, :]
        gap = jnp.where(own < LIMIT, own - mean, 0.0)
        square = square + jnp.sum((gap * gap).reshape(8, 8, BLK), axis=0)
    spread = jnp.sum(jnp.sum(square, axis=0, keepdims=True), axis=1, keepdims=True)

    line[pl.ds(z, 1), :] = as_row(count, mean, spread)
    pl.semaphore_wait(barrier, 7 + z + y)

    def send(buf, slot, sem, to):
        pltpu.make_async_remote_copy(
            src_ref=buf.at[pl.ds(slot, 1)], dst_ref=buf.at[pl.ds(slot, 1)],
            send_sem=sem.at[0], recv_sem=sem.at[1],
            device_id=to, device_id_type=MESH).start()

    def send_line(k):
        send(line, z, z_sem, on_line(k))

    each(0, z, send_line)
    each(0, z, lambda k: signal(here.at[0], on_line(k)))

    mate = g + 1 - 2 * lax.rem(g, 2)
    right, left, far = lax.rem(g + 2, 8), lax.rem(g + 6, 8), lax.rem(g + 4, 8)
    low, high, whole = pl.ds(0, HALF), pl.ds(HALF, HALF), pl.ds(0, ROWS)

    def move(i, owner, span, to):
        copy = pltpu.make_async_remote_copy(
            src_ref=gath.at[owner, span], dst_ref=gath.at[owner, span],
            send_sem=data_send.at[i], recv_sem=data_recv.at[i],
            device_id=(d, to), device_id_type=MESH)
        copy.start()
        return copy

    r1 = move(0, g, low, right)
    l1 = move(1, g, high, left)
    r2 = move(2, g, high, right)
    l2 = move(3, g, low, left)
    own = move(4, g, whole, mate)

    each(0, y, lambda k: signal(here.at[1], on_row(k)))

    for i in range(NBLK):
        col = slice(i * BLK, (i + 1) * BLK)
        for h in range(2):
            seqs = slice(h * 8, h * 8 + 8)
            adv = gath[g, h * HALF + i * 8:h * HALF + i * 8 + 8, :]
            ret[seqs, col] = jnp.where(adv < LIMIT, adv + val[seqs, col], 0.0)

    r1.wait_recv()
    r3 = move(5, left, low, right)
    l1.wait_recv()
    l3 = move(6, right, high, left)
    m1 = move(7, left, low, mate)
    m2 = move(8, right, high, mate)
    await_signals(here.at[1], 7 - y)
    each(y + 1, 8, lambda k: signal(here.at[2], on_row(k)))
    await_signals(here.at[0], 7 - z)
    each(z + 1, 8, send_line)
    others_z = line.at[pl.ds(0, 7)]
    pltpu.make_async_copy(others_z, others_z, z_sem.at[1]).wait()
    mine = y * 8 + g
    plane[pl.ds(mine, 1), :] = as_row(*merged(line[...]))
    await_signals(here.at[2], y)
    def send_plane(k):
        send(plane, mine, plane_sem, on_plane(k))

    each(0, mine, send_plane)
    each(mine + 1, 64, send_plane)

    r2.wait_recv()
    m3 = move(9, left, high, mate)
    l2.wait_recv()
    m4 = move(10, right, low, mate)

    r3.wait_recv()
    m5 = move(11, far, low, mate)
    l3.wait_recv()
    m6 = move(12, far, high, mate)
    for copy in (own, m1, m2, m3, m4, m5, m6):
        copy.wait_recv()

    loads[4].wait()

    def gather(i, _):
        for j in range(16):
            slot = i * 16 + j
            want = asg[0, slot]
            row = ((want & 31) << 3) | ((want >> 5) & 7)
            rows[pl.ds(slot, 1), :] = gath[want >> 9, pl.ds((want & 256) + row, 1), :]
        return 0

    lax.fori_loop(0, ROWS // 16, gather, 0)

    others = plane.at[pl.ds(0, 63)]
    pltpu.make_async_copy(others, others, plane_sem.at[1]).wait()
    n, middle, deviation = merged(plane[...])
    stats[0:1, :] = middle
    stats[1:2, :] = lax.rsqrt(deviation / n + EPSILON)
    pltpu.make_async_copy(others, others, plane_sem.at[0]).wait()
    pltpu.make_async_copy(others_z, others_z, z_sem.at[0]).wait()
    for copy in [r1, l1, r2, l2, own, r3, l3, m1, m2, m3, m4, m5, m6]:
        copy.wait_send()


def finish(ret, rows, stats, ret_hbm, train_hbm, train, sem):
    give_returns = pltpu.make_async_copy(ret, ret_hbm, sem.at[0])
    give_returns.start()
    middle, scale = stats[0:1, :], stats[1:2, :]
    gives = []
    for i in range(2):
        part = slice(i * HALF, (i + 1) * HALF)
        picked = rows[part, :]
        train[part, :] = jnp.where(picked < LIMIT, (picked - middle) * scale, 0.0)
        give = pltpu.make_async_copy(train.at[part], train_hbm.at[part], sem.at[1 + i])
        give.start()
        gives.append(give)
    give_returns.wait()
    for give in gives:
        give.wait()


def body(rewards, values, horizon, lengths, assignment):
    hbm = pl.BlockSpec(memory_space=pltpu.MemorySpace.HBM)
    f32 = jnp.float32
    vmem = pl.BlockSpec(memory_space=pltpu.MemorySpace.VMEM)
    ret, rows, stats = pl.pallas_call(
        kernel,
        out_shape=tuple(jax.ShapeDtypeStruct(shape, f32) for shape in ((SEQ, LEN), (ROWS, BLK), (8, BLK))),
        in_specs=[hbm] * 5,
        out_specs=(vmem, vmem, vmem),
        scratch_shapes=[
            pltpu.VMEM((SEQ, LEN), f32),
            pltpu.VMEM((SEQ, LEN), f32),
            pltpu.VMEM((1, SEQ), f32),
            pltpu.VMEM((1, SEQ), jnp.int32),
            pltpu.SMEM((1, ROWS), jnp.int32),
            pltpu.VMEM((8, ROWS, BLK), f32),
            pltpu.VMEM((64, BLK), f32),
            pltpu.VMEM((8, BLK), f32),
            pltpu.SemaphoreType.DMA((5,)),
            pltpu.SemaphoreType.DMA((2,)),
            pltpu.SemaphoreType.DMA((2,)),
            pltpu.SemaphoreType.REGULAR((3,)),
            pltpu.SemaphoreType.DMA((13,)),
            pltpu.SemaphoreType.DMA((13,)),
        ],
        compiler_params=pltpu.CompilerParams(collective_id=0, has_side_effects=True, vmem_limit_bytes=16 << 20),
        name="advantage",
    )(*(pltpu.with_memory_space_constraint(x, pltpu.MemorySpace.HBM) for x in (rewards, values, horizon.reshape(1, SEQ), lengths.reshape(1, SEQ), assignment)))
    return pl.pallas_call(
        finish,
        out_shape=(jax.ShapeDtypeStruct((SEQ, LEN), f32), jax.ShapeDtypeStruct((ROWS, BLK), f32)),
        in_specs=[vmem] * 3,
        out_specs=(hbm, hbm),
        scratch_shapes=[pltpu.VMEM((ROWS, BLK), f32), pltpu.SemaphoreType.DMA((3,))],
        compiler_params=pltpu.CompilerParams(vmem_limit_bytes=4 << 20),
        name="finish",
    )(ret, rows, stats)


def solution(mesh):
    in_specs = (
        P(("dp", "group"), None),
        P(("dp", "group"), None),
        P(("dp", "group")),
        P(("dp", "group")),
        P("dp", "group"),
    )
    out_specs = (P(("dp", "group"), None), P(("dp", "group"), None))
    return jax.shard_map(body, mesh=mesh, in_specs=in_specs, out_specs=out_specs, check_vma=False)
```

```python
import jax
import jax.numpy as jnp
from jax import lax
from jax.experimental import pallas as pl
from jax.experimental.pallas import tpu as pltpu
from jax.sharding import PartitionSpec as P

LEN = 4096
BLK = 128
SEQ = 16
NBLK = LEN // BLK
ROWS = SEQ * NBLK
HALF = ROWS // 2
TRACE_DECAY = 0.998
MORE = 1.0 / TRACE_DECAY - 1.0
EPSILON = 1e-05
OUTSIDE = 1e30
LIMIT = 1e29
CHUNK = 8
MESH = pl.DeviceIdType.MESH


def column(row):
    wide = jnp.broadcast_to(row, (SEQ, SEQ))
    down = lax.broadcasted_iota(jnp.int32, (SEQ, SEQ), 0)
    across = lax.broadcasted_iota(jnp.int32, (SEQ, SEQ), 1)
    picked = jnp.sum(jnp.where(down == across, wide, 0.0), axis=1, keepdims=True)
    return jnp.broadcast_to(picked, (SEQ, BLK))


def as_row(count, mean, spread):
    lane = lax.broadcasted_iota(jnp.int32, (1, BLK), 1)
    return jnp.where(lane == 0, count, jnp.where(lane == 1, mean, spread))


def merged(rows):
    n, m, s = (jnp.broadcast_to(rows[:, j:j + 1], rows.shape) for j in range(3))
    total = jnp.sum(n, axis=0, keepdims=True)
    mean = jnp.sum(n * m, axis=0, keepdims=True) / total
    gap = m - mean
    spread = jnp.sum(s + n * gap * gap, axis=0, keepdims=True)
    return total, mean, spread


def each(first, last, act):
    lax.fori_loop(first, last, lambda k, c: (act(k), c)[1], 0)


def kernel(rew_hbm, val_hbm, hor_hbm, len_hbm, asg_hbm, ret, rows, stats,
           rew, val, hor, lens, wants, asg, gath, plane, line,
           in_sem, plane_sem, z_sem, here, above, data_send, data_recv):
    d = lax.axis_index("dp")
    g = lax.axis_index("group")
    y, z = lax.rem(d, 8), d // 8

    def signal(sem, where):
        pl.semaphore_signal(sem, inc=1, device_id=where, device_id_type=MESH)

    def await_signals(sem, count):
        @pl.when(count > 0)
        def _():
            pl.semaphore_wait(sem, count)

    def on_line(k):
        return k * 8 + y, g

    def on_row(k):
        return z * 8 + k, g

    def on_plane(k):
        return z * 8 + k // 8, lax.rem(k, 8)

    loads = [
        pltpu.make_async_copy(src, dst, in_sem.at[i])
        for i, (src, dst) in enumerate(
            [(hor_hbm, hor), (len_hbm, lens), (val_hbm, val), (rew_hbm, rew), (asg_hbm, wants)])
    ]
    for load in loads:
        load.start()

    barrier = pltpu.get_barrier_semaphore()
    each(z + 1, 8, lambda k: signal(barrier, on_line(z + 8 - k)))
    each(y + 1, 8, lambda k: signal(barrier, on_row(y + 8 - k)))
    for k in (4, 3, 5, 2, 6, 1, 7):
        signal(barrier, (d, lax.rem(g + k, 8)))

    loads[0].wait()
    loads[1].wait()

    lane = lax.broadcasted_iota(jnp.int32, (SEQ, BLK), 1)
    length = column(lens[...].astype(jnp.float32)).astype(jnp.int32)
    gamma = 1.0 - 1.0 / column(hor[...])
    power = gamma * TRACE_DECAY
    rise = jnp.ones((SEQ, BLK), jnp.float32)
    for k in range(7):
        rise = rise * jnp.where(((lane >> k) & 1) == 1, power, 1.0)
        power = power * power
    fall = 1.0 / rise
    down = lax.broadcasted_iota(jnp.int32, (BLK, 2 * BLK), 0)
    across = lax.broadcasted_iota(jnp.int32, (BLK, 2 * BLK), 1)
    ones = jnp.where((across >= BLK) | (down >= across), 1.0, 0.0).astype(jnp.bfloat16)
    twice = jnp.concatenate([ones, ones], axis=0)
    past = lane - length
    zero = jnp.zeros((SEQ, BLK), jnp.float32)
    carry, total = zero, zero
    shape = (CHUNK, SEQ, BLK)
    loads[2].wait()
    loads[3].wait()
    for first in range(NBLK - CHUNK, -1, -CHUNK):
        cols = [slice((first + i) * BLK, (first + i + 1) * BLK) for i in range(CHUNK)]
        v = jnp.stack([val[:, c] for c in cols])
        r = jnp.stack([rew[:, c] for c in cols])
        inside = jnp.stack([past < -(first + i) * BLK for i in range(CHUNK)])
        part = jnp.where(inside, r + MORE * v, 0.0)
        scaled = (part * rise[None]).reshape(CHUNK * SEQ, BLK)
        high = scaled.astype(jnp.bfloat16)
        rest = scaled - high.astype(jnp.float32)
        middle = rest.astype(jnp.bfloat16)
        low = (rest - middle.astype(jnp.float32)).astype(jnp.bfloat16)
        sums = jnp.dot(jnp.concatenate([high, middle], axis=1), twice, preferred_element_type=jnp.float32)
        sums = sums + jnp.dot(low, ones, preferred_element_type=jnp.float32)
        inner, whole_block = sums[:, :BLK].reshape(shape), sums[:, BLK:].reshape(shape)
        for i in range(CHUNK - 1, -1, -1):
            tail = power * carry
            adv = (inner[i] + tail) * fall - (1.0 + MORE) * v[i]
            carry = whole_block[i] + tail
            total = total + jnp.where(inside[i], adv, 0.0)
            sent = jnp.where(inside[i], adv, OUTSIDE)
            at = (first + i) * 8
            gath[g, at:at + 8, :] = sent[:8]
            gath[g, HALF + at:HALF + at + 8, :] = sent[8:]

    count = jnp.sum(jnp.sum(length[:, 0:1].astype(jnp.float32), axis=0, keepdims=True), axis=1, keepdims=True)
    mean = jnp.sum(jnp.sum(total, axis=0, keepdims=True), axis=1, keepdims=True) / count
    square = jnp.zeros((8, BLK), jnp.float32)
    for i in range(ROWS // 64):
        own = gath[g, i * 64:(i + 1) * 64, :]
        gap = jnp.where(own < LIMIT, own - mean, 0.0)
        square = square + jnp.sum((gap * gap).reshape(8, 8, BLK), axis=0)
    spread = jnp.sum(jnp.sum(square, axis=0, keepdims=True), axis=1, keepdims=True)

    line[pl.ds(z, 1), :] = as_row(count, mean, spread)
    pl.semaphore_wait(barrier, 7 + z + y)

    def send(buf, slot, sem, to):
        pltpu.make_async_remote_copy(
            src_ref=buf.at[pl.ds(slot, 1)], dst_ref=buf.at[pl.ds(slot, 1)],
            send_sem=sem.at[0], recv_sem=sem.at[1],
            device_id=to, device_id_type=MESH).start()

    def send_line(k):
        send(line, z, z_sem, on_line(k))

    each(0, z, send_line)
    each(0, z, lambda k: signal(above.at[z], on_line(k)))

    mate = g + 1 - 2 * lax.rem(g, 2)
    right, left, far = lax.rem(g + 2, 8), lax.rem(g + 6, 8), lax.rem(g + 4, 8)
    low, high, whole = pl.ds(0, HALF), pl.ds(HALF, HALF), pl.ds(0, ROWS)

    def move(i, owner, span, to):
        copy = pltpu.make_async_remote_copy(
            src_ref=gath.at[owner, span], dst_ref=gath.at[owner, span],
            send_sem=data_send.at[i], recv_sem=data_recv.at[i],
            device_id=(d, to), device_id_type=MESH)
        copy.start()
        return copy

    r1 = move(0, g, low, right)
    l1 = move(1, g, high, left)
    r2 = move(2, g, high, right)
    l2 = move(3, g, low, left)
    own = move(4, g, whole, mate)

    each(0, y, lambda k: signal(here.at[0], on_row(k)))

    loads[4].wait()
    want = wants[...]
    wants[...] = (want - lax.rem(want, 256)) + lax.rem(want, 32) * 8 + lax.rem(want // 32, 8)

    for i in range(NBLK):
        col = slice(i * BLK, (i + 1) * BLK)
        for h in range(2):
            seqs = slice(h * 8, h * 8 + 8)
            adv = gath[g, h * HALF + i * 8:h * HALF + i * 8 + 8, :]
            ret[seqs, col] = jnp.where(adv < LIMIT, adv + val[seqs, col], 0.0)

    number = pltpu.make_async_copy(wants, asg, in_sem.at[5])
    number.start()

    r1.wait_recv()
    r3 = move(5, left, low, right)
    l1.wait_recv()
    l3 = move(6, right, high, left)
    m1 = move(7, left, low, mate)
    m2 = move(8, right, high, mate)
    await_signals(here.at[0], 7 - y)
    each(y + 1, 8, lambda k: signal(here.at[1], on_row(k)))

    def send_up(k):
        pl.semaphore_wait(above.at[k], 1)
        send_line(k)

    each(z + 1, 8, send_up)
    others_z = line.at[pl.ds(0, 7)]
    pltpu.make_async_copy(others_z, others_z, z_sem.at[1]).wait()
    mine = y * 8 + g
    plane[pl.ds(mine, 1), :] = as_row(*merged(line[...]))
    await_signals(here.at[1], y)

    def send_plane(k):
        send(plane, mine, plane_sem, on_plane(k))

    for k in range(8):
        pl.when(mine != k)(lambda k=k: send_plane(k))
    each(8, mine, send_plane)
    each(lax.max(mine + 1, 8), 64, send_plane)

    r2.wait_recv()
    m3 = move(9, left, high, mate)
    l2.wait_recv()
    m4 = move(10, right, low, mate)

    r3.wait_recv()
    m5 = move(11, far, low, mate)
    l3.wait_recv()
    m6 = move(12, far, high, mate)
    for copy in (own, m1, m2, m3, m4, m5, m6):
        copy.wait_recv()

    number.wait()

    flat = gath.reshape(8 * ROWS, BLK)

    def gather(i, _):
        for j in range(16):
            slot = i * 16 + j
            rows[pl.ds(slot, 1), :] = flat[pl.ds(asg[0, slot], 1), :]
        return 0

    lax.fori_loop(0, ROWS // 16, gather, 0)

    others = plane.at[pl.ds(0, 63)]
    pltpu.make_async_copy(others, others, plane_sem.at[1]).wait()
    n, middle, deviation = merged(plane[...])
    stats[0:1, :] = middle
    stats[1:2, :] = lax.rsqrt(deviation / n + EPSILON)
    pltpu.make_async_copy(others, others, plane_sem.at[0]).wait()
    pltpu.make_async_copy(others_z, others_z, z_sem.at[0]).wait()
    for copy in [r1, l1, r2, l2, own, r3, l3, m1, m2, m3, m4, m5, m6]:
        copy.wait_send()


def finish(ret, rows, stats, ret_hbm, train_hbm, train, sem):
    give_returns = pltpu.make_async_copy(ret, ret_hbm, sem.at[0])
    give_returns.start()
    middle, scale = stats[0:1, :], stats[1:2, :]
    gives = []
    for i in range(2):
        part = slice(i * HALF, (i + 1) * HALF)
        picked = rows[part, :]
        train[part, :] = jnp.where(picked < LIMIT, (picked - middle) * scale, 0.0)
        give = pltpu.make_async_copy(train.at[part], train_hbm.at[part], sem.at[1 + i])
        give.start()
        gives.append(give)
    give_returns.wait()
    for give in gives:
        give.wait()


def body(rewards, values, horizon, lengths, assignment):
    hbm = pl.BlockSpec(memory_space=pltpu.MemorySpace.HBM)
    f32 = jnp.float32
    vmem = pl.BlockSpec(memory_space=pltpu.MemorySpace.VMEM)
    ret, rows, stats = pl.pallas_call(
        kernel,
        out_shape=tuple(jax.ShapeDtypeStruct(shape, f32) for shape in ((SEQ, LEN), (ROWS, BLK), (8, BLK))),
        in_specs=[hbm] * 5,
        out_specs=(vmem, vmem, vmem),
        scratch_shapes=[
            pltpu.VMEM((SEQ, LEN), f32),
            pltpu.VMEM((SEQ, LEN), f32),
            pltpu.VMEM((1, SEQ), f32),
            pltpu.VMEM((1, SEQ), jnp.int32),
            pltpu.VMEM((1, ROWS), jnp.int32),
            pltpu.SMEM((1, ROWS), jnp.int32),
            pltpu.VMEM((8, ROWS, BLK), f32),
            pltpu.VMEM((64, BLK), f32),
            pltpu.VMEM((8, BLK), f32),
            pltpu.SemaphoreType.DMA((6,)),
            pltpu.SemaphoreType.DMA((2,)),
            pltpu.SemaphoreType.DMA((2,)),
            pltpu.SemaphoreType.REGULAR((2,)),
            pltpu.SemaphoreType.REGULAR((8,)),
            pltpu.SemaphoreType.DMA((13,)),
            pltpu.SemaphoreType.DMA((13,)),
        ],
        compiler_params=pltpu.CompilerParams(collective_id=0, has_side_effects=True, vmem_limit_bytes=16 << 20),
        name="advantage",
    )(*(pltpu.with_memory_space_constraint(x, pltpu.MemorySpace.HBM) for x in (rewards, values, horizon.reshape(1, SEQ), lengths.reshape(1, SEQ), assignment)))
    return pl.pallas_call(
        finish,
        out_shape=(jax.ShapeDtypeStruct((SEQ, LEN), f32), jax.ShapeDtypeStruct((ROWS, BLK), f32)),
        in_specs=[vmem] * 3,
        out_specs=(hbm, hbm),
        scratch_shapes=[pltpu.VMEM((ROWS, BLK), f32), pltpu.SemaphoreType.DMA((3,))],
        compiler_params=pltpu.CompilerParams(vmem_limit_bytes=4 << 20),
        name="finish",
    )(ret, rows, stats)


def solution(mesh):
    in_specs = (
        P(("dp", "group"), None),
        P(("dp", "group"), None),
        P(("dp", "group")),
        P(("dp", "group")),
        P("dp", "group"),
    )
    out_specs = (P(("dp", "group"), None), P(("dp", "group"), None))
    return jax.shard_map(body, mesh=mesh, in_specs=in_specs, out_specs=out_specs, check_vma=False)
```

```python
import jax
import jax.numpy as jnp
from jax import lax
from jax.experimental import pallas as pl
from jax.experimental.pallas import tpu as pltpu
from jax.sharding import PartitionSpec as P

LEN = 4096
BLK = 128
SEQ = 16
NBLK = LEN // BLK
ROWS = SEQ * NBLK
HALF = ROWS // 2
TRACE_DECAY = 0.998
MORE = 1.0 / TRACE_DECAY - 1.0
EPSILON = 1e-05
OUTSIDE = 1e30
LIMIT = 1e29
CHUNK = 8
MESH = pl.DeviceIdType.MESH


def column(row):
    wide = jnp.broadcast_to(row, (SEQ, SEQ))
    down = lax.broadcasted_iota(jnp.int32, (SEQ, SEQ), 0)
    across = lax.broadcasted_iota(jnp.int32, (SEQ, SEQ), 1)
    picked = jnp.sum(jnp.where(down == across, wide, 0.0), axis=1, keepdims=True)
    return jnp.broadcast_to(picked, (SEQ, BLK))


def as_row(count, mean, spread):
    lane = lax.broadcasted_iota(jnp.int32, (1, BLK), 1)
    return jnp.where(lane == 0, count, jnp.where(lane == 1, mean, spread))


def merged(rows):
    n, m, s = (jnp.broadcast_to(rows[:, j:j + 1], rows.shape) for j in range(3))
    total = jnp.sum(n, axis=0, keepdims=True)
    mean = jnp.sum(n * m, axis=0, keepdims=True) / total
    gap = m - mean
    spread = jnp.sum(s + n * gap * gap, axis=0, keepdims=True)
    return total, mean, spread


def each(first, last, act):
    lax.fori_loop(first, last, lambda k, c: (act(k), c)[1], 0)


def kernel(rew_hbm, val_hbm, hor_hbm, len_hbm, asg_hbm, ret, rows, stats,
           rew, val, hor, lens, wants, asg, gath, plane, line,
           in_sem, plane_sem, z_sem, here, above, data_send, data_recv):
    d = lax.axis_index("dp")
    g = lax.axis_index("group")
    y, z = lax.rem(d, 8), d // 8

    def signal(sem, where):
        pl.semaphore_signal(sem, inc=1, device_id=where, device_id_type=MESH)

    def await_signals(sem, count):
        @pl.when(count > 0)
        def _():
            pl.semaphore_wait(sem, count)

    core = lax.rem(g, 2)

    def on_line(k):
        return k // 2 * 8 + y, g - core + lax.rem(k, 2)

    def on_row(k):
        return z * 8 + k, g

    def on_plane(k):
        return z * 8 + k // 4, lax.rem(k, 4) * 2 + core

    loads = [
        pltpu.make_async_copy(src, dst, in_sem.at[i])
        for i, (src, dst) in enumerate(
            [(hor_hbm, hor), (len_hbm, lens), (val_hbm, val), (rew_hbm, rew), (asg_hbm, wants)])
    ]
    for load in loads:
        load.start()

    barrier = pltpu.get_barrier_semaphore()
    each(2 * z + 2, 16, lambda k: signal(barrier, on_line(2 * z + 17 - k)))
    each(y + 1, 8, lambda k: signal(barrier, on_row(y + 8 - k)))
    for k in (4, 3, 5, 2, 6, 1, 7):
        signal(barrier, (d, lax.rem(g + k, 8)))

    loads[0].wait()
    loads[1].wait()

    lane = lax.broadcasted_iota(jnp.int32, (SEQ, BLK), 1)
    length = column(lens[...].astype(jnp.float32)).astype(jnp.int32)
    gamma = 1.0 - 1.0 / column(hor[...])
    power = gamma * TRACE_DECAY
    rise = jnp.ones((SEQ, BLK), jnp.float32)
    for k in range(7):
        rise = rise * jnp.where(((lane >> k) & 1) == 1, power, 1.0)
        power = power * power
    fall = 1.0 / rise
    down = lax.broadcasted_iota(jnp.int32, (BLK, 2 * BLK), 0)
    across = lax.broadcasted_iota(jnp.int32, (BLK, 2 * BLK), 1)
    ones = jnp.where((across >= BLK) | (down >= across), 1.0, 0.0).astype(jnp.bfloat16)
    twice = jnp.concatenate([ones, ones], axis=0)
    past = lane - length
    zero = jnp.zeros((SEQ, BLK), jnp.float32)
    carry, total = zero, zero
    shape = (CHUNK, SEQ, BLK)
    loads[2].wait()
    loads[3].wait()
    for first in range(NBLK - CHUNK, -1, -CHUNK):
        cols = [slice((first + i) * BLK, (first + i + 1) * BLK) for i in range(CHUNK)]
        v = jnp.stack([val[:, c] for c in cols])
        r = jnp.stack([rew[:, c] for c in cols])
        inside = jnp.stack([past < -(first + i) * BLK for i in range(CHUNK)])
        part = jnp.where(inside, r + MORE * v, 0.0)
        scaled = (part * rise[None]).reshape(CHUNK * SEQ, BLK)
        high = scaled.astype(jnp.bfloat16)
        rest = scaled - high.astype(jnp.float32)
        middle = rest.astype(jnp.bfloat16)
        low = (rest - middle.astype(jnp.float32)).astype(jnp.bfloat16)
        sums = jnp.dot(jnp.concatenate([high, middle], axis=1), twice, preferred_element_type=jnp.float32)
        sums = sums + jnp.dot(low, ones, preferred_element_type=jnp.float32)
        inner, whole_block = sums[:, :BLK].reshape(shape), sums[:, BLK:].reshape(shape)
        for i in range(CHUNK - 1, -1, -1):
            tail = power * carry
            adv = (inner[i] + tail) * fall - (1.0 + MORE) * v[i]
            carry = whole_block[i] + tail
            total = total + jnp.where(inside[i], adv, 0.0)
            sent = jnp.where(inside[i], adv, OUTSIDE)
            at = (first + i) * 8
            gath[g, at:at + 8, :] = sent[:8]
            gath[g, HALF + at:HALF + at + 8, :] = sent[8:]

    count = jnp.sum(jnp.sum(length[:, 0:1].astype(jnp.float32), axis=0, keepdims=True), axis=1, keepdims=True)
    mean = jnp.sum(jnp.sum(total, axis=0, keepdims=True), axis=1, keepdims=True) / count
    square = jnp.zeros((8, BLK), jnp.float32)
    for i in range(ROWS // 64):
        own = gath[g, i * 64:(i + 1) * 64, :]
        gap = jnp.where(own < LIMIT, own - mean, 0.0)
        square = square + jnp.sum((gap * gap).reshape(8, 8, BLK), axis=0)
    spread = jnp.sum(jnp.sum(square, axis=0, keepdims=True), axis=1, keepdims=True)

    spot = 2 * z + core
    line[pl.ds(spot, 1), :] = as_row(count, mean, spread)
    pl.semaphore_wait(barrier, 7 + 2 * z + y)

    def send(buf, slot, sem, to):
        pltpu.make_async_remote_copy(
            src_ref=buf.at[pl.ds(slot, 1)], dst_ref=buf.at[pl.ds(slot, 1)],
            send_sem=sem.at[0], recv_sem=sem.at[1],
            device_id=to, device_id_type=MESH).start()

    def send_line(k):
        send(line, spot, z_sem, on_line(k))

    each(0, 2 * z, send_line)
    send_line(spot + 1 - 2 * core)
    each(0, 2 * z, lambda k: signal(above.at[spot], on_line(k)))

    mate = g + 1 - 2 * lax.rem(g, 2)
    right, left, far = lax.rem(g + 2, 8), lax.rem(g + 6, 8), lax.rem(g + 4, 8)
    low, high, whole = pl.ds(0, HALF), pl.ds(HALF, HALF), pl.ds(0, ROWS)

    def move(i, owner, span, to):
        copy = pltpu.make_async_remote_copy(
            src_ref=gath.at[owner, span], dst_ref=gath.at[owner, span],
            send_sem=data_send.at[i], recv_sem=data_recv.at[i],
            device_id=(d, to), device_id_type=MESH)
        copy.start()
        return copy

    r1 = move(0, g, low, right)
    l1 = move(1, g, high, left)
    r2 = move(2, g, high, right)
    l2 = move(3, g, low, left)
    own = move(4, g, whole, mate)

    each(0, y, lambda k: signal(here.at[0], on_row(k)))

    loads[4].wait()
    want = wants[...]
    wants[...] = (want - lax.rem(want, 256)) + lax.rem(want, 32) * 8 + lax.rem(want // 32, 8)

    for i in range(NBLK):
        col = slice(i * BLK, (i + 1) * BLK)
        for h in range(2):
            seqs = slice(h * 8, h * 8 + 8)
            adv = gath[g, h * HALF + i * 8:h * HALF + i * 8 + 8, :]
            ret[seqs, col] = jnp.where(adv < LIMIT, adv + val[seqs, col], 0.0)

    number = pltpu.make_async_copy(wants, asg, in_sem.at[5])
    number.start()

    r1.wait_recv()
    r3 = move(5, left, low, right)
    l1.wait_recv()
    l3 = move(6, right, high, left)
    m1 = move(7, left, low, mate)
    m2 = move(8, right, high, mate)
    await_signals(here.at[0], 7 - y)
    each(y + 1, 8, lambda k: signal(here.at[1], on_row(k)))

    def send_up(k):
        pl.semaphore_wait(above.at[k], 1)
        send_line(k)

    each(2 * z + 2, 16, send_up)
    others_z = line.at[pl.ds(0, 15)]
    pltpu.make_async_copy(others_z, others_z, z_sem.at[1]).wait()
    mine = y * 4 + g // 2
    plane[pl.ds(mine, 1), :] = as_row(*merged(line[...]))
    await_signals(here.at[1], y)

    def send_plane(k):
        send(plane, mine, plane_sem, on_plane(k))

    for k in range(4):
        pl.when(mine != k)(lambda k=k: send_plane(k))
    each(4, mine, send_plane)
    each(lax.max(mine + 1, 4), 32, send_plane)

    r2.wait_recv()
    m3 = move(9, left, high, mate)
    l2.wait_recv()
    m4 = move(10, right, low, mate)

    r3.wait_recv()
    m5 = move(11, far, low, mate)
    l3.wait_recv()
    m6 = move(12, far, high, mate)
    for copy in (own, m1, m2, m3, m4, m5, m6):
        copy.wait_recv()

    number.wait()

    flat = gath.reshape(8 * ROWS, BLK)

    def gather(i, _):
        for j in range(16):
            slot = i * 16 + j
            rows[pl.ds(slot, 1), :] = flat[pl.ds(asg[0, slot], 1), :]
        return 0

    lax.fori_loop(0, ROWS // 16, gather, 0)

    others = plane.at[pl.ds(0, 31)]
    pltpu.make_async_copy(others, others, plane_sem.at[1]).wait()
    n, middle, deviation = merged(plane[...])
    stats[0:1, :] = middle
    stats[1:2, :] = lax.rsqrt(deviation / n + EPSILON)
    pltpu.make_async_copy(others, others, plane_sem.at[0]).wait()
    pltpu.make_async_copy(others_z, others_z, z_sem.at[0]).wait()
    for copy in [r1, l1, r2, l2, own, r3, l3, m1, m2, m3, m4, m5, m6]:
        copy.wait_send()


def finish(ret, rows, stats, ret_hbm, train_hbm, train, sem):
    give_returns = pltpu.make_async_copy(ret, ret_hbm, sem.at[0])
    give_returns.start()
    middle, scale = stats[0:1, :], stats[1:2, :]
    gives = []
    for i in range(2):
        part = slice(i * HALF, (i + 1) * HALF)
        picked = rows[part, :]
        train[part, :] = jnp.where(picked < LIMIT, (picked - middle) * scale, 0.0)
        give = pltpu.make_async_copy(train.at[part], train_hbm.at[part], sem.at[1 + i])
        give.start()
        gives.append(give)
    give_returns.wait()
    for give in gives:
        give.wait()


def body(rewards, values, horizon, lengths, assignment):
    hbm = pl.BlockSpec(memory_space=pltpu.MemorySpace.HBM)
    f32 = jnp.float32
    vmem = pl.BlockSpec(memory_space=pltpu.MemorySpace.VMEM)
    ret, rows, stats = pl.pallas_call(
        kernel,
        out_shape=tuple(jax.ShapeDtypeStruct(shape, f32) for shape in ((SEQ, LEN), (ROWS, BLK), (8, BLK))),
        in_specs=[hbm] * 5,
        out_specs=(vmem, vmem, vmem),
        scratch_shapes=[
            pltpu.VMEM((SEQ, LEN), f32),
            pltpu.VMEM((SEQ, LEN), f32),
            pltpu.VMEM((1, SEQ), f32),
            pltpu.VMEM((1, SEQ), jnp.int32),
            pltpu.VMEM((1, ROWS), jnp.int32),
            pltpu.SMEM((1, ROWS), jnp.int32),
            pltpu.VMEM((8, ROWS, BLK), f32),
            pltpu.VMEM((32, BLK), f32),
            pltpu.VMEM((16, BLK), f32),
            pltpu.SemaphoreType.DMA((6,)),
            pltpu.SemaphoreType.DMA((2,)),
            pltpu.SemaphoreType.DMA((2,)),
            pltpu.SemaphoreType.REGULAR((2,)),
            pltpu.SemaphoreType.REGULAR((16,)),
            pltpu.SemaphoreType.DMA((13,)),
            pltpu.SemaphoreType.DMA((13,)),
        ],
        compiler_params=pltpu.CompilerParams(collective_id=0, has_side_effects=True, vmem_limit_bytes=16 << 20),
        name="advantage",
    )(*(pltpu.with_memory_space_constraint(x, pltpu.MemorySpace.HBM) for x in (rewards, values, horizon.reshape(1, SEQ), lengths.reshape(1, SEQ), assignment)))
    return pl.pallas_call(
        finish,
        out_shape=(jax.ShapeDtypeStruct((SEQ, LEN), f32), jax.ShapeDtypeStruct((ROWS, BLK), f32)),
        in_specs=[vmem] * 3,
        out_specs=(hbm, hbm),
        scratch_shapes=[pltpu.VMEM((ROWS, BLK), f32), pltpu.SemaphoreType.DMA((3,))],
        compiler_params=pltpu.CompilerParams(vmem_limit_bytes=4 << 20),
        name="finish",
    )(ret, rows, stats)


def solution(mesh):
    in_specs = (
        P(("dp", "group"), None),
        P(("dp", "group"), None),
        P(("dp", "group")),
        P(("dp", "group")),
        P("dp", "group"),
    )
    out_specs = (P(("dp", "group"), None), P(("dp", "group"), None))
    return jax.shard_map(body, mesh=mesh, in_specs=in_specs, out_specs=out_specs, check_vma=False)
```

```python
import jax
import jax.numpy as jnp
from jax import lax
from jax.experimental import pallas as pl
from jax.experimental.pallas import tpu as pltpu
from jax.sharding import PartitionSpec as P

LEN = 4096
BLK = 128
SEQ = 16
NBLK = LEN // BLK
ROWS = SEQ * NBLK
HALF = ROWS // 2
TRACE_DECAY = 0.998
MORE = 1.0 / TRACE_DECAY - 1.0
EPSILON = 1e-05
OUTSIDE = 1e30
LIMIT = 1e29
CHUNK = 8
MESH = pl.DeviceIdType.MESH


def column(row):
    wide = jnp.broadcast_to(row, (SEQ, SEQ))
    down = lax.broadcasted_iota(jnp.int32, (SEQ, SEQ), 0)
    across = lax.broadcasted_iota(jnp.int32, (SEQ, SEQ), 1)
    picked = jnp.sum(jnp.where(down == across, wide, 0.0), axis=1, keepdims=True)
    return jnp.broadcast_to(picked, (SEQ, BLK))


def as_row(count, mean, spread):
    lane = lax.broadcasted_iota(jnp.int32, (1, BLK), 1)
    return jnp.where(lane == 0, count, jnp.where(lane == 1, mean, spread))


def merged(rows):
    n, m, s = (jnp.broadcast_to(rows[:, j:j + 1], rows.shape) for j in range(3))
    total = jnp.sum(n, axis=0, keepdims=True)
    mean = jnp.sum(n * m, axis=0, keepdims=True) / total
    gap = m - mean
    spread = jnp.sum(s + n * gap * gap, axis=0, keepdims=True)
    return total, mean, spread


def each(first, last, act):
    lax.fori_loop(first, last, lambda k, c: (act(k), c)[1], 0)


def kernel(rew_hbm, val_hbm, hor_hbm, len_hbm, asg_hbm, ret, rows, stats,
           rew, val, hor, lens, wants, asg, gath, plane, line,
           in_sem, plane_sem, z_sem, here, above, data_send, data_recv):
    d = lax.axis_index("dp")
    g = lax.axis_index("group")
    y, z = lax.rem(d, 8), d // 8

    def signal(sem, where):
        pl.semaphore_signal(sem, inc=1, device_id=where, device_id_type=MESH)

    def await_signals(sem, count):
        @pl.when(count > 0)
        def _():
            pl.semaphore_wait(sem, count)

    core = lax.rem(g, 2)

    def on_line(k):
        return k // 2 * 8 + y, g - core + lax.rem(k, 2)

    def on_row(k):
        return z * 8 + k, g

    def on_plane(k):
        return z * 8 + k // 4, lax.rem(k, 4) * 2 + core

    loads = [
        pltpu.make_async_copy(src, dst, in_sem.at[i])
        for i, (src, dst) in enumerate(
            [(hor_hbm, hor), (len_hbm, lens), (val_hbm, val), (rew_hbm, rew), (asg_hbm, wants)])
    ]
    for load in loads:
        load.start()

    barrier = pltpu.get_barrier_semaphore()
    each(2 * z + 2, 16, lambda k: signal(barrier, on_line(2 * z + 17 - k)))
    each(y + 1, 8, lambda k: signal(barrier, on_row(y + 8 - k)))
    for k in (4, 3, 5, 2, 6, 1, 7):
        signal(barrier, (d, lax.rem(g + k, 8)))

    loads[0].wait()
    loads[1].wait()

    lane = lax.broadcasted_iota(jnp.int32, (SEQ, BLK), 1)
    length = column(lens[...].astype(jnp.float32)).astype(jnp.int32)
    gamma = 1.0 - 1.0 / column(hor[...])
    power = gamma * TRACE_DECAY
    rise = jnp.ones((SEQ, BLK), jnp.float32)
    for k in range(7):
        rise = rise * jnp.where(((lane >> k) & 1) == 1, power, 1.0)
        power = power * power
    fall = 1.0 / rise
    down = lax.broadcasted_iota(jnp.int32, (BLK, 2 * BLK), 0)
    across = lax.broadcasted_iota(jnp.int32, (BLK, 2 * BLK), 1)
    ones = jnp.where((across >= BLK) | (down >= across), 1.0, 0.0).astype(jnp.bfloat16)
    twice = jnp.concatenate([ones, ones], axis=0)
    past = lane - length
    zero = jnp.zeros((SEQ, BLK), jnp.float32)
    carry, total = zero, zero
    shape = (CHUNK, SEQ, BLK)
    loads[2].wait()
    loads[3].wait()
    for first in range(NBLK - CHUNK, -1, -CHUNK):
        cols = [slice((first + i) * BLK, (first + i + 1) * BLK) for i in range(CHUNK)]
        v = jnp.stack([val[:, c] for c in cols])
        r = jnp.stack([rew[:, c] for c in cols])
        inside = jnp.stack([past < -(first + i) * BLK for i in range(CHUNK)])
        part = jnp.where(inside, r + MORE * v, 0.0)
        scaled = (part * rise[None]).reshape(CHUNK * SEQ, BLK)
        high = scaled.astype(jnp.bfloat16)
        rest = scaled - high.astype(jnp.float32)
        middle = rest.astype(jnp.bfloat16)
        low = (rest - middle.astype(jnp.float32)).astype(jnp.bfloat16)
        sums = jnp.dot(jnp.concatenate([high, middle], axis=1), twice, preferred_element_type=jnp.float32)
        sums = sums + jnp.dot(low, ones, preferred_element_type=jnp.float32)
        inner, whole_block = sums[:, :BLK].reshape(shape), sums[:, BLK:].reshape(shape)
        for i in range(CHUNK - 1, -1, -1):
            tail = power * carry
            adv = (inner[i] + tail) * fall - (1.0 + MORE) * v[i]
            carry = whole_block[i] + tail
            total = total + jnp.where(inside[i], adv, 0.0)
            sent = jnp.where(inside[i], adv, OUTSIDE)
            at = (first + i) * 8
            gath[g, at:at + 8, :] = sent[:8]
            gath[g, HALF + at:HALF + at + 8, :] = sent[8:]

    count = jnp.sum(jnp.sum(length[:, 0:1].astype(jnp.float32), axis=0, keepdims=True), axis=1, keepdims=True)
    mean = jnp.sum(jnp.sum(total, axis=0, keepdims=True), axis=1, keepdims=True) / count
    square = jnp.zeros((8, BLK), jnp.float32)
    for i in range(ROWS // 64):
        own = gath[g, i * 64:(i + 1) * 64, :]
        gap = jnp.where(own < LIMIT, own - mean, 0.0)
        square = square + jnp.sum((gap * gap).reshape(8, 8, BLK), axis=0)
    spread = jnp.sum(jnp.sum(square, axis=0, keepdims=True), axis=1, keepdims=True)

    spot = 2 * z + core
    line[pl.ds(spot, 1), :] = as_row(count, mean, spread)
    pl.semaphore_wait(barrier, 7 + 2 * z + y)

    def send(buf, slot, sem, to):
        pltpu.make_async_remote_copy(
            src_ref=buf.at[pl.ds(slot, 1)], dst_ref=buf.at[pl.ds(slot, 1)],
            send_sem=sem.at[0], recv_sem=sem.at[1],
            device_id=to, device_id_type=MESH).start()

    def send_line(k):
        send(line, spot, z_sem, on_line(k))

    each(0, 2 * z, send_line)
    send_line(spot + 1 - 2 * core)
    each(0, 2 * z, lambda k: signal(above.at[spot], on_line(k)))

    mate = g + 1 - 2 * lax.rem(g, 2)
    right, left, far = lax.rem(g + 2, 8), lax.rem(g + 6, 8), lax.rem(g + 4, 8)
    low, high, whole = pl.ds(0, HALF), pl.ds(HALF, HALF), pl.ds(0, ROWS)

    def move(i, owner, span, to):
        copy = pltpu.make_async_remote_copy(
            src_ref=gath.at[owner, span], dst_ref=gath.at[owner, span],
            send_sem=data_send.at[i], recv_sem=data_recv.at[i],
            device_id=(d, to), device_id_type=MESH)
        copy.start()
        return copy

    r1 = move(0, g, low, right)
    l1 = move(1, g, high, left)
    r2 = move(2, g, high, right)
    l2 = move(3, g, low, left)
    own = move(4, g, whole, mate)

    each(0, y, lambda k: signal(here.at[0], on_row(k)))

    loads[4].wait()
    want = wants[...]
    wants[...] = (want - lax.rem(want, 256)) + lax.rem(want, 32) * 8 + lax.rem(want // 32, 8)

    for i in range(NBLK):
        col = slice(i * BLK, (i + 1) * BLK)
        for h in range(2):
            seqs = slice(h * 8, h * 8 + 8)
            adv = gath[g, h * HALF + i * 8:h * HALF + i * 8 + 8, :]
            ret[seqs, col] = jnp.where(adv < LIMIT, adv + val[seqs, col], 0.0)

    number = pltpu.make_async_copy(wants, asg, in_sem.at[5])
    number.start()

    r1.wait_recv()
    r3 = move(5, left, low, right)
    l1.wait_recv()
    l3 = move(6, right, high, left)
    m1 = move(7, left, low, mate)
    m2 = move(8, right, high, mate)
    await_signals(here.at[0], 7 - y)
    each(y + 1, 8, lambda k: signal(here.at[1], on_row(k)))

    def send_up(k):
        pl.semaphore_wait(above.at[k], 1)
        send_line(k)

    each(2 * z + 2, 16, send_up)
    others_z = line.at[pl.ds(0, 15)]
    pltpu.make_async_copy(others_z, others_z, z_sem.at[1]).wait()
    mine = y * 4 + g // 2
    plane[pl.ds(mine, 1), :] = as_row(*merged(line[...]))
    await_signals(here.at[1], y)

    def send_plane(k):
        send(plane, mine, plane_sem, on_plane(k))

    for k in range(32):
        pl.when(mine != k)(lambda k=k: send_plane(k))

    r2.wait_recv()
    m3 = move(9, left, high, mate)
    l2.wait_recv()
    m4 = move(10, right, low, mate)

    r3.wait_recv()
    m5 = move(11, far, low, mate)
    l3.wait_recv()
    m6 = move(12, far, high, mate)
    for copy in (own, m1, m2, m3, m4, m5, m6):
        copy.wait_recv()

    number.wait()

    flat = gath.reshape(8 * ROWS, BLK)

    def gather(i, _):
        for j in range(16):
            slot = i * 16 + j
            rows[pl.ds(slot, 1), :] = flat[pl.ds(asg[0, slot], 1), :]
        return 0

    lax.fori_loop(0, ROWS // 16, gather, 0)

    others = plane.at[pl.ds(0, 31)]
    pltpu.make_async_copy(others, others, plane_sem.at[1]).wait()
    n, middle, deviation = merged(plane[...])
    stats[0:1, :] = middle
    stats[1:2, :] = lax.rsqrt(deviation / n + EPSILON)
    pltpu.make_async_copy(others, others, plane_sem.at[0]).wait()
    pltpu.make_async_copy(others_z, others_z, z_sem.at[0]).wait()
    for copy in [r1, l1, r2, l2, own, r3, l3, m1, m2, m3, m4, m5, m6]:
        copy.wait_send()


def finish(ret, rows, stats, ret_hbm, train_hbm, train, sem):
    give_returns = pltpu.make_async_copy(ret, ret_hbm, sem.at[0])
    give_returns.start()
    middle, scale = stats[0:1, :], stats[1:2, :]
    gives = []
    for i in range(2):
        part = slice(i * HALF, (i + 1) * HALF)
        picked = rows[part, :]
        train[part, :] = jnp.where(picked < LIMIT, (picked - middle) * scale, 0.0)
        give = pltpu.make_async_copy(train.at[part], train_hbm.at[part], sem.at[1 + i])
        give.start()
        gives.append(give)
    give_returns.wait()
    for give in gives:
        give.wait()


def body(rewards, values, horizon, lengths, assignment):
    hbm = pl.BlockSpec(memory_space=pltpu.MemorySpace.HBM)
    f32 = jnp.float32
    vmem = pl.BlockSpec(memory_space=pltpu.MemorySpace.VMEM)
    ret, rows, stats = pl.pallas_call(
        kernel,
        out_shape=tuple(jax.ShapeDtypeStruct(shape, f32) for shape in ((SEQ, LEN), (ROWS, BLK), (8, BLK))),
        in_specs=[hbm] * 5,
        out_specs=(vmem, vmem, vmem),
        scratch_shapes=[
            pltpu.VMEM((SEQ, LEN), f32),
            pltpu.VMEM((SEQ, LEN), f32),
            pltpu.VMEM((1, SEQ), f32),
            pltpu.VMEM((1, SEQ), jnp.int32),
            pltpu.VMEM((1, ROWS), jnp.int32),
            pltpu.SMEM((1, ROWS), jnp.int32),
            pltpu.VMEM((8, ROWS, BLK), f32),
            pltpu.VMEM((32, BLK), f32),
            pltpu.VMEM((16, BLK), f32),
            pltpu.SemaphoreType.DMA((6,)),
            pltpu.SemaphoreType.DMA((2,)),
            pltpu.SemaphoreType.DMA((2,)),
            pltpu.SemaphoreType.REGULAR((2,)),
            pltpu.SemaphoreType.REGULAR((16,)),
            pltpu.SemaphoreType.DMA((13,)),
            pltpu.SemaphoreType.DMA((13,)),
        ],
        compiler_params=pltpu.CompilerParams(collective_id=0, has_side_effects=True, vmem_limit_bytes=16 << 20),
        name="advantage",
    )(*(pltpu.with_memory_space_constraint(x, pltpu.MemorySpace.HBM) for x in (rewards, values, horizon.reshape(1, SEQ), lengths.reshape(1, SEQ), assignment)))
    return pl.pallas_call(
        finish,
        out_shape=(jax.ShapeDtypeStruct((SEQ, LEN), f32), jax.ShapeDtypeStruct((ROWS, BLK), f32)),
        in_specs=[vmem] * 3,
        out_specs=(hbm, hbm),
        scratch_shapes=[pltpu.VMEM((ROWS, BLK), f32), pltpu.SemaphoreType.DMA((3,))],
        compiler_params=pltpu.CompilerParams(vmem_limit_bytes=4 << 20),
        name="finish",
    )(ret, rows, stats)


def solution(mesh):
    in_specs = (
        P(("dp", "group"), None),
        P(("dp", "group"), None),
        P(("dp", "group")),
        P(("dp", "group")),
        P("dp", "group"),
    )
    out_specs = (P(("dp", "group"), None), P(("dp", "group"), None))
    return jax.shard_map(body, mesh=mesh, in_specs=in_specs, out_specs=out_specs, check_vma=False)
```
